256 devices in a mesh: section: 16 (over z, core), ctx: 16 (over x, y).
Axes of the slice: x: 4, y: 4, z: 8, core: 2. Of those that a mesh axis runs over, the one named last changes fastest.
Arguments:
- queries: bfloat16 [16, 2560, 32, 128], P('section', 'ctx'), may hold values from -30 to 30
- key_rows: bfloat16 [16, 2560, 16, 128], P('section', 'ctx'), may hold values from -6 to 6
- stored_value_rows: bfloat16 [16, 2560, 16, 128], P('section', 'ctx'), may hold values from -6 to 6
- grad_out: bfloat16 [16, 2560, 32, 128], P('section', 'ctx'), may hold values from -6 to 6
Outputs:
- query_gradient_rows: bfloat16 [16, 2560, 32, 128], P('section', 'ctx')
- grad_keys: bfloat16 [16, 2560, 16, 128], P('section', 'ctx')
- grad_values: bfloat16 [16, 2560, 16, 128], P('section', 'ctx')
The draws below stay inside these ranges and needn't reach their ends.
All inputs are finite; a program needn't handle non-finite values.
Results may differ from the reference program's by a relative error of at most 0.009.
Values may be sent and summed in bfloat16 or wider, within the bound.
A program may use at most 128 MiB of HBM per device.

```python
import jax
import jax.numpy as jnp
from jax import lax

HQ = 32
KEY_VALUE_HEADS = 16
HEAD_WIDTH = 128
WINDOW = 1024
QBLOCK = 256
RELAY_SECTIONS = 16
SECTION_TOKENS = 2560


def draw_queries(key, part):
    sampled_values = jax.random.truncated_normal(jax.random.fold_in(key, 1), -6.0, 6.0, (RELAY_SECTIONS, SECTION_TOKENS, HQ, HEAD_WIDTH), jnp.float32)
    return sampled_values.astype(jnp.bfloat16)


def draw_key_rows(key, part):
    sampled_values = jax.random.truncated_normal(jax.random.fold_in(key, 2), -6.0, 6.0, (RELAY_SECTIONS, SECTION_TOKENS, KEY_VALUE_HEADS, HEAD_WIDTH), jnp.float32)
    return sampled_values.astype(jnp.bfloat16)


def level_of(stream_key, extent, pieces, low, top_value):
    def one(dim, shards_of):
        heights = jax.random.uniform(jax.random.fold_in(jax.random.fold_in(stream_key, 6), dim), (shards_of,), jnp.float32, low / len(pieces), top_value / len(pieces))
        return jnp.repeat(jnp.exp(heights), extent[dim] // shards_of).reshape((-1,) + (1,) * (len(extent) - dim - 1))

    gain = one(*pieces[0])
    for cut in pieces[1:]:
        gain = gain * one(*cut)
    return gain


def gaussian(rng, dims, deviation, most, cuts=(), kind=jnp.bfloat16):
    loudness = level_of(rng, dims, cuts, -0.22, 0.18) if cuts else 1.0
    result = jax.random.normal(rng, dims, jnp.float32) * deviation * loudness
    return jnp.minimum(jnp.maximum(result, -most), most).astype(kind)


def setup_inputs(seed: int = 0) -> dict:
    arg_keys = jax.random.split(jax.random.key(seed), 5)
    return {
        "queries": draw_queries(jax.random.fold_in(arg_keys[4], 71), 0),
        "key_rows": draw_key_rows(jax.random.fold_in(arg_keys[4], 71), 0),
        "stored_value_rows": gaussian(arg_keys[2], (RELAY_SECTIONS, SECTION_TOKENS, KEY_VALUE_HEADS, HEAD_WIDTH), 1.0, 6.0, ((0, 16), (1, 16))),
        "grad_out": gaussian(arg_keys[3], (RELAY_SECTIONS, SECTION_TOKENS, HQ, HEAD_WIDTH), 1.0, 6.0, ((0, 16), (1, 16))),
    }


query_scale = 168.0 ** -0.5
masked_value = -1.0e30


def group_grads(query_group, key_group, value_group, grad_group):
    length = query_group.shape[0]
    per_group = query_group.shape[1]
    head_size = query_group.shape[2]
    padding = jnp.zeros((WINDOW, head_size), jnp.bfloat16)
    key_all = jnp.concatenate([padding, key_group], axis=0)
    value_all = jnp.concatenate([padding, value_group], axis=0)
    span = QBLOCK + WINDOW
    high = lax.Precision.HIGHEST

    def one_block(block_num, carry):
        grad_query_all, key_gradient_total, grad_value_acc = carry
        first_row = (block_num * QBLOCK).astype(jnp.int32)
        query_block = lax.dynamic_slice_in_dim(query_group, first_row, QBLOCK, 0).astype(jnp.float32)
        grad_block = lax.dynamic_slice_in_dim(grad_group, first_row, QBLOCK, 0).astype(jnp.float32)
        key_block = lax.dynamic_slice_in_dim(key_all, first_row, span, 0).astype(jnp.float32)
        value_block = lax.dynamic_slice_in_dim(value_all, first_row, span, 0).astype(jnp.float32)
        query_places = first_row + jnp.arange(QBLOCK, dtype=jnp.int32)
        key_places = first_row - WINDOW + jnp.arange(span, dtype=jnp.int32)
        allowed = (key_places[None, :] <= query_places[:, None]) & (key_places[None, :] > query_places[:, None] - WINDOW) & (key_places[None, :] >= 0)
        scores = jnp.einsum("bgd,kd->gbk", query_block, key_block, precision=high) * query_scale
        scores = jnp.where(allowed, scores, masked_value)
        row_max = jnp.max(scores, axis=-1, keepdims=True)
        weights = jnp.exp(scores - row_max)
        probs_full = weights / jnp.sum(weights, axis=-1, keepdims=True)
        probs_half = probs_full.astype(jnp.bfloat16).astype(jnp.float32)
        grad_probs = jnp.einsum("bgd,kd->gbk", grad_block, value_block, precision=high)
        row_dot = jnp.sum(probs_full * grad_probs, axis=-1, keepdims=True)
        grad_scores = (probs_full * (grad_probs - row_dot)).astype(jnp.bfloat16).astype(jnp.float32)
        grad_query = jnp.einsum("gbk,kd->bgd", grad_scores, key_block, precision=high) * query_scale
        grad_key = jnp.einsum("gbk,bgd->kd", grad_scores, query_block, precision=high) * query_scale
        grad_value = jnp.einsum("gbk,bgd->kd", probs_half, grad_block, precision=high)
        grad_query_all = lax.dynamic_update_slice_in_dim(grad_query_all, grad_query.astype(jnp.bfloat16), first_row, 0)
        old_keys = lax.dynamic_slice_in_dim(key_gradient_total, first_row, span, 0)
        key_gradient_total = lax.dynamic_update_slice_in_dim(key_gradient_total, old_keys + grad_key, first_row, 0)
        old_values = lax.dynamic_slice_in_dim(grad_value_acc, first_row, span, 0)
        grad_value_acc = lax.dynamic_update_slice_in_dim(grad_value_acc, old_values + grad_value, first_row, 0)
        return grad_query_all, key_gradient_total, grad_value_acc

    start_state = (jnp.zeros((length, per_group, head_size), jnp.bfloat16),
                   jnp.zeros((length + WINDOW, head_size), jnp.float32),
                   jnp.zeros((length + WINDOW, head_size), jnp.float32))
    finals = lax.fori_loop(0, length // QBLOCK, one_block, start_state)
    return finals[0], finals[1][WINDOW:].astype(jnp.bfloat16), finals[2][WINDOW:].astype(jnp.bfloat16)


def reference(queries, key_rows, stored_value_rows, grad_out):
    incoming = jnp.roll(grad_out, -1, axis=0)
    sections, length, heads, head_size = queries.shape
    kv_heads = key_rows.shape[2]
    per_group = heads // kv_heads

    def regroup(array):
        shaped = array.reshape(sections, length, kv_heads, per_group, head_size).transpose(0, 2, 1, 3, 4)
        return shaped.reshape(sections * kv_heads, length, per_group, head_size)

    def regroup_pairs(array):
        return array.transpose(0, 2, 1, 3).reshape(sections * kv_heads, length, head_size)

    outputs = lax.map(lambda items: group_grads(*items),
                      (regroup(queries), regroup_pairs(key_rows), regroup_pairs(stored_value_rows), regroup(incoming)))
    query_gradient_rows = outputs[0].reshape(sections, kv_heads, length, per_group, head_size).transpose(0, 2, 1, 3, 4).reshape(sections, length, heads, head_size)
    grad_keys = outputs[1].reshape(sections, kv_heads, length, head_size).transpose(0, 2, 1, 3)
    grad_values = outputs[2].reshape(sections, kv_heads, length, head_size).transpose(0, 2, 1, 3)
    return (query_gradient_rows, grad_keys, grad_values)
```

```python
import functools
import math

import jax
import jax.numpy as jnp
from jax import lax
from jax.experimental import pallas as pl
from jax.experimental.pallas import tpu as pltpu
from jax.sharding import PartitionSpec as P

MESH = pl.DeviceIdType.MESH
WINDOW = 1024
BLOCK = 128
BIG = 1e30
query_scale = 168.0 ** (-0.5)
exponent_scale = query_scale * math.log2(math.e)

F32 = jnp.float32
BF16 = jnp.bfloat16


def contract(left, right, dims):
    return lax.dot_general(left, right, (dims, ((), ())), preferred_element_type=F32)


def kernel(
    sections,
    members,
    q_hbm,
    k_hbm,
    v_hbm,
    g_hbm,
    dq_hbm,
    dk_hbm,
    dv_hbm,
    q_all,
    k_all,
    v_all,
    g_all,
    k_cols,
    weights,
    grad_probs,
    half_probs,
    grad_scores,
    norms,
    dk_sum,
    dv_sum,
    dq_all,
    dk_all,
    dv_all,
    in_send,
    in_recv,
    out_send,
    out_recv,
):
    section = lax.axis_index("section")
    me = lax.axis_index("ctx")
    side = math.isqrt(members)
    my_x, my_y = me // side, me % side
    rows = q_hbm.shape[0]
    length = rows * members
    per_group = q_hbm.shape[2]
    blocks = length // BLOCK
    tiles = WINDOW // BLOCK + 1
    span = WINDOW + BLOCK
    lanes = per_group * BLOCK
    behind = (section + sections - 1) % sections
    ahead = (section + 1) % sections

    def peer(step):
        x = (my_x + step // side) % side
        y = (my_y + step % side) % side
        return x * side + y

    barrier = pltpu.get_barrier_semaphore()

    def greet(step, carry):
        pl.semaphore_signal(
            barrier, inc=1, device_id=(ahead, peer(step)), device_id_type=MESH
        )

        @pl.when(step > 0)
        def _():
            pl.semaphore_signal(
                barrier, inc=1, device_id=(section, peer(step)), device_id_type=MESH
            )

        return carry

    lax.fori_loop(0, members, greet, 0)
    pl.semaphore_wait(barrier, 2 * members - 1)

    def place(buffer, who, pad):
        return buffer.at[pl.ds(pad + who * rows, rows)]

    def inbound(number, source, buffer, pad):
        def send(step, carry):
            who = peer(step)

            @pl.when(step == 0)
            def _():
                pltpu.make_async_copy(
                    source(who), place(buffer, me, pad), in_recv.at[number]
                ).start()

            @pl.when(step > 0)
            def _():
                pltpu.make_async_remote_copy(
                    src_ref=source(who),
                    dst_ref=place(buffer, me, pad),
                    send_sem=in_send.at[number],
                    recv_sem=in_recv.at[number],
                    device_id=(section, who),
                    device_id_type=MESH,
                ).start()

            return carry

        lax.fori_loop(0, members, send, 0)

    inbound(0, lambda who: k_hbm.at[who], k_all, WINDOW)
    inbound(1, lambda who: q_hbm.at[:, who], q_all, 0)
    inbound(2, lambda who: v_hbm.at[who], v_all, WINDOW)

    def send_grad(step, carry):
        who = peer(step)
        pltpu.make_async_remote_copy(
            src_ref=g_hbm.at[:, who],
            dst_ref=place(g_all, me, 0),
            send_sem=in_send.at[3],
            recv_sem=in_recv.at[3],
            device_id=(behind, who),
            device_id_type=MESH,
        ).start()
        return carry

    lax.fori_loop(0, members, send_grad, 0)

    def await_bytes(view, semaphore):
        pltpu.make_async_copy(view, view, semaphore).wait()

    k_all[0:WINDOW, :] = jnp.zeros((WINDOW, k_all.shape[1]), BF16)
    v_all[0:WINDOW, :] = jnp.zeros((WINDOW, v_all.shape[1]), BF16)
    dk_sum[...] = jnp.zeros(dk_sum.shape, F32)
    dv_sum[...] = jnp.zeros(dv_sum.shape, F32)

    q_rows = q_all.reshape(length * per_group, q_all.shape[2])
    g_rows = g_all.reshape(length * per_group, g_all.shape[2])
    dq_rows = dq_all.reshape(length * per_group, dq_all.shape[2])

    await_bytes(k_all.at[pl.ds(WINDOW, length)], in_recv.at[0])

    def turn(tile, carry):
        first = pl.multiple_of(tile * BLOCK, BLOCK)
        k_cols[:, pl.ds(first, BLOCK)] = k_all[pl.ds(first, BLOCK), :].T
        return carry

    lax.fori_loop(0, (length + WINDOW) // BLOCK, turn, 0)
    await_bytes(q_all, in_recv.at[1])

    def weigh(block, carry):
        first = pl.multiple_of(block * BLOCK, BLOCK)
        query = q_rows[pl.ds(pl.multiple_of(block * lanes, lanes), lanes), :]
        scores = contract(k_all[pl.ds(first, span), :], query, ((1,), (1,)))
        key_place = lax.broadcasted_iota(jnp.int32, (BLOCK, lanes), 0)
        query_place = lax.broadcasted_iota(jnp.int32, (BLOCK, lanes), 1) // per_group
        tops = []
        for tile in range(tiles):
            part = scores[tile * BLOCK : (tile + 1) * BLOCK, :]
            if tile == 0:
                part = jnp.where(key_place > query_place, part, -BIG)
            if tile == tiles - 1:
                part = jnp.where(key_place <= query_place, part, -BIG)
            weights[block, tile * BLOCK : (tile + 1) * BLOCK, :] = part
            top = jnp.max(part, axis=0, keepdims=True)
            tops.append(jnp.where(tile + block >= tiles - 1, top, -BIG))
        row_max = functools.reduce(jnp.maximum, tops)
        total = jnp.zeros((1, lanes), F32)
        for tile in range(tiles):
            level = jnp.where(tile + block >= tiles - 1, row_max, BIG)
            part = weights[block, tile * BLOCK : (tile + 1) * BLOCK, :]
            part = jnp.exp2((part - level) * exponent_scale)
            weights[block, tile * BLOCK : (tile + 1) * BLOCK, :] = part
            total = total + jnp.sum(part, axis=0, keepdims=True)
        norms[block] = 1.0 / total
        return carry

    lax.fori_loop(0, blocks, weigh, 0)

    await_bytes(v_all.at[pl.ds(WINDOW, length)], in_recv.at[2])
    await_bytes(g_all, in_recv.at[3])

    groups = 4
    group_blocks = blocks // groups
    group_members = members // groups

    def home(step):
        return (my_x + 1 + step // group_blocks) % groups

    def send_query_grads(step):
        who = home(step) * group_members + step % group_blocks - 1
        source = dq_all.at[pl.ds(who * rows, rows)]

        @pl.when(who == me)
        def _():
            pltpu.make_async_copy(source, dq_hbm.at[:, me], out_recv.at[0]).start()

        @pl.when(who != me)
        def _():
            pltpu.make_async_remote_copy(
                src_ref=source,
                dst_ref=dq_hbm.at[:, me],
                send_sem=out_send.at[0],
                recv_sem=out_recv.at[0],
                device_id=(section, who),
                device_id_type=MESH,
            ).start()

    def grads(step, carry):
        block = home(step) * group_blocks + step % group_blocks
        first = pl.multiple_of(block * BLOCK, BLOCK)
        window = pl.ds(first, span)
        band = pl.ds(pl.multiple_of(block * lanes, lanes), lanes)
        incoming = g_rows[band, :]
        norm = norms[block]
        products = contract(v_all[window, :], incoming, ((1,), (1,)))
        row_dot = jnp.zeros((1, lanes), F32)
        for tile in range(tiles):
            cut = slice(tile * BLOCK, (tile + 1) * BLOCK)
            part = products[cut, :]
            probs = weights[block, cut, :] * norm
            half_probs[cut, :] = probs.astype(BF16)
            grad_probs[cut, :] = part
            row_dot = row_dot + jnp.sum(probs * part, axis=0, keepdims=True)
        for tile in range(tiles):
            cut = slice(tile * BLOCK, (tile + 1) * BLOCK)
            probs = weights[block, cut, :] * norm
            grad_scores[cut, :] = (probs * (grad_probs[cut, :] - row_dot)).astype(BF16)
        dv_sum[window, :] += contract(half_probs[...], incoming, ((1,), (0,)))
        dk_sum[window, :] += contract(grad_scores[...], q_rows[band, :], ((1,), (0,)))
        turned = contract(k_cols[:, window], grad_scores[...], ((1,), (0,)))
        dq_rows[band, :] = (turned * query_scale).T.astype(BF16)

        @pl.when((step > 0) & ((step + group_blocks - 1) % group_blocks > 0))
        def _():
            send_query_grads(step - 1)

        return carry

    lax.fori_loop(0, blocks, grads, 0)
    send_query_grads(blocks - 1)

    def finish(block, carry):
        here = pl.ds(pl.multiple_of(block * BLOCK, BLOCK), BLOCK)
        there = pl.ds(pl.multiple_of(WINDOW + block * BLOCK, BLOCK), BLOCK)
        dk_all[here, :] = (dk_sum[there, :] * query_scale).astype(BF16)
        dv_all[here, :] = dv_sum[there, :].astype(BF16)
        return carry

    lax.fori_loop(0, blocks, finish, 0)

    def outbound(number, source, target):
        def send(step, carry):
            who = peer(step)
            mine = source.at[pl.ds(who * rows, rows)]

            @pl.when(step == 0)
            def _():
                pltpu.make_async_copy(mine, target.at[me], out_recv.at[number]).start()

            @pl.when(step > 0)
            def _():
                pltpu.make_async_remote_copy(
                    src_ref=mine,
                    dst_ref=target.at[me],
                    send_sem=out_send.at[number],
                    recv_sem=out_recv.at[number],
                    device_id=(section, who),
                    device_id_type=MESH,
                ).start()

            return carry

        lax.fori_loop(0, members, send, 0)

    outbound(1, dv_all, dv_hbm)
    outbound(2, dk_all, dk_hbm)

    others = pl.ds(0, length - rows)
    await_bytes(k_all.at[others], in_send.at[0])
    await_bytes(q_all.at[others], in_send.at[1])
    await_bytes(v_all.at[others], in_send.at[2])
    await_bytes(g_all, in_send.at[3])
    await_bytes(dq_all.at[others], out_send.at[0])
    await_bytes(dv_all.at[others], out_send.at[1])
    await_bytes(dk_all.at[others], out_send.at[2])
    await_bytes(dq_all, out_recv.at[0])
    await_bytes(dv_all, out_recv.at[1])
    await_bytes(dk_all, out_recv.at[2])


def solution(mesh):
    sections, members = mesh.shape["section"], mesh.shape["ctx"]

    def body(queries, key_rows, stored_value_rows, grad_out):
        _, rows, heads, width = queries.shape
        groups = key_rows.shape[2]
        per_group = heads // groups
        length = rows * members
        blocks = length // BLOCK
        span = WINDOW + BLOCK
        lanes = per_group * BLOCK
        by_group = (rows, groups, per_group, width)
        anywhere = pl.BlockSpec(memory_space=pl.ANY)
        dq, dk, dv = pl.pallas_call(
            functools.partial(kernel, sections, members),
            out_shape=(
                jax.ShapeDtypeStruct(by_group, BF16),
                jax.ShapeDtypeStruct((groups, rows, width), BF16),
                jax.ShapeDtypeStruct((groups, rows, width), BF16),
            ),
            in_specs=[anywhere] * 4,
            out_specs=(anywhere,) * 3,
            scratch_shapes=[
                pltpu.VMEM((length, per_group, width), BF16),
                pltpu.VMEM((length + WINDOW, width), BF16),
                pltpu.VMEM((length + WINDOW, width), BF16),
                pltpu.VMEM((length, per_group, width), BF16),
                pltpu.VMEM((width, length + WINDOW), BF16),
                pltpu.VMEM((blocks, span, lanes), F32),
                pltpu.VMEM((span, lanes), F32),
                pltpu.VMEM((span, lanes), BF16),
                pltpu.VMEM((span, lanes), BF16),
                pltpu.VMEM((blocks, 1, lanes), F32),
                pltpu.VMEM((length + WINDOW, width), F32),
                pltpu.VMEM((length + WINDOW, width), F32),
                pltpu.VMEM((length, per_group, width), BF16),
                pltpu.VMEM((length, width), BF16),
                pltpu.VMEM((length, width), BF16),
                pltpu.SemaphoreType.DMA((4,)),
                pltpu.SemaphoreType.DMA((4,)),
                pltpu.SemaphoreType.DMA((3,)),
                pltpu.SemaphoreType.DMA((3,)),
            ],
            compiler_params=pltpu.CompilerParams(
                collective_id=0, has_side_effects=True, vmem_limit_bytes=60 << 20
            ),
            name="relay_attention_backward",
        )(
            queries.reshape(by_group),
            key_rows[0].transpose(1, 0, 2),
            stored_value_rows[0].transpose(1, 0, 2),
            grad_out.reshape(by_group),
        )
        return (
            dq.reshape(1, rows, heads, width),
            dk.transpose(1, 0, 2)[None],
            dv.transpose(1, 0, 2)[None],
        )

    spec = P("section", "ctx", None, None)
    return jax.shard_map(
        body, mesh=mesh, in_specs=(spec,) * 4, out_specs=(spec,) * 3, check_vma=False
    )
```

```python
import functools
import math

import jax
import jax.numpy as jnp
from jax import lax
from jax.experimental import pallas as pl
from jax.experimental.pallas import tpu as pltpu
from jax.sharding import PartitionSpec as P

MESH = pl.DeviceIdType.MESH
WINDOW = 1024
BLOCK = 128
CHUNK = 32
BIG = 1e30
query_scale = 168.0 ** (-0.5)
exponent_scale = query_scale * math.log2(math.e)

F32 = jnp.float32
BF16 = jnp.bfloat16


def contract(left, right, dims):
    return lax.dot_general(left, right, (dims, ((), ())), preferred_element_type=F32)


def kernel(
    sections,
    members,
    q_hbm,
    k_hbm,
    v_hbm,
    g_hbm,
    dq_out,
    dk_out,
    dv_out,
    q_all,
    k_all,
    v_all,
    g_all,
    k_cols,
    weights,
    norms,
    grad_probs,
    next_probs,
    grad_scores,
    dk_sum,
    dv_sum,
    dq_all,
    dk_all,
    dv_all,
    q_raw,
    k_raw,
    v_raw,
    g_raw,
    q_ready,
    k_ready,
    v_ready,
    g_ready,
    dq_back,
    dk_back,
    dv_back,
    wide,
    load_sem,
    in_send,
    in_recv,
    out_send,
    out_recv,
):
    section = lax.axis_index("section")
    me = lax.axis_index("ctx")
    side = math.isqrt(members)
    my_x, my_y = me // side, me % side
    rows = q_hbm.shape[0]
    length = rows * members
    heads, groups = q_hbm.shape[1], k_hbm.shape[1]
    per_group = heads // groups
    blocks = length // BLOCK
    tiles = WINDOW // BLOCK + 1
    span = WINDOW + BLOCK
    lanes = per_group * BLOCK
    behind = (section + sections - 1) % sections
    ahead = (section + 1) % sections

    def peer(step):
        x = (my_x + step) % side
        y = (my_y + step // side + step) % side
        return x * side + y

    loads = [
        pltpu.make_async_copy(source, raw, load_sem.at[number])
        for number, (source, raw) in enumerate(
            ((k_hbm, k_raw), (q_hbm, q_raw), (v_hbm, v_raw), (g_hbm, g_raw))
        )
    ]
    for load in loads:
        load.start()

    barrier = pltpu.get_barrier_semaphore()

    def greet(step, carry):
        pl.semaphore_signal(
            barrier, inc=1, device_id=(ahead, peer(step)), device_id_type=MESH
        )

        @pl.when(step > 0)
        def _():
            pl.semaphore_signal(
                barrier, inc=1, device_id=(section, peer(step)), device_id_type=MESH
            )

        return carry

    lax.fori_loop(0, members, greet, 0)

    def by_group(raw, ready):
        count = raw.shape[1]
        each = count // groups
        flat = raw.reshape(rows * count, raw.shape[2])

        def one(chunk, carry):
            here = pl.ds(pl.multiple_of(chunk * CHUNK * count, CHUNK), CHUNK * count)
            wide[0 : CHUNK * count, :] = flat[here, :].astype(F32)
            for head in range(count):
                first = (chunk * each + head % each) * CHUNK
                ready[head // each, pl.ds(pl.multiple_of(first, CHUNK), CHUNK), :] = (
                    wide[pl.ds(head, CHUNK, stride=count), :].astype(BF16)
                )
            return carry

        lax.fori_loop(0, rows // CHUNK, one, 0)

    def by_row(back, out):
        count = out.shape[1]
        each = count // groups
        flat = out.reshape(rows * count, out.shape[2])

        def one(chunk, carry):
            for head in range(count):
                first = (chunk * each + head % each) * CHUNK
                wide[pl.ds(head, CHUNK, stride=count), :] = back[
                    head // each, pl.ds(pl.multiple_of(first, CHUNK), CHUNK), :
                ].astype(F32)
            here = pl.ds(pl.multiple_of(chunk * CHUNK * count, CHUNK), CHUNK * count)
            flat[here, :] = wide[0 : CHUNK * count, :].astype(BF16)
            return carry

        lax.fori_loop(0, rows // CHUNK, one, 0)

    loads[0].wait()
    by_group(k_raw, k_ready)
    pl.semaphore_wait(barrier, 2 * members - 1)

    def inbound(number, ready, buffer, pad, target_section):
        size = ready.shape[1]
        there = buffer.at[pl.ds(pad + me * size, size)]

        def send(step, carry):
            who = peer(step)
            near = (step == 0) & (target_section == section)

            @pl.when(near)
            def _():
                pltpu.make_async_copy(
                    ready.at[who], there, in_recv.at[number]
                ).start()

            @pl.when(jnp.logical_not(near))
            def _():
                pltpu.make_async_remote_copy(
                    src_ref=ready.at[who],
                    dst_ref=there,
                    send_sem=in_send.at[number],
                    recv_sem=in_recv.at[number],
                    device_id=(target_section, who),
                    device_id_type=MESH,
                ).start()

            return carry

        lax.fori_loop(0, members, send, 0)

    inbound(0, k_ready, k_all, WINDOW, section)
    loads[1].wait()
    by_group(q_raw, q_ready)
    inbound(1, q_ready, q_all, 0, section)
    loads[2].wait()
    by_group(v_raw, v_ready)
    inbound(2, v_ready, v_all, WINDOW, section)
    loads[3].wait()
    by_group(g_raw, g_ready)
    inbound(3, g_ready, g_all, 0, behind)

    def await_bytes(view, semaphore):
        pltpu.make_async_copy(view, view, semaphore).wait()

    k_all[0:WINDOW, :] = jnp.zeros((WINDOW, k_all.shape[1]), BF16)
    v_all[0:WINDOW, :] = jnp.zeros((WINDOW, v_all.shape[1]), BF16)
    dk_sum[...] = jnp.zeros(dk_sum.shape, F32)
    dv_sum[...] = jnp.zeros(dv_sum.shape, F32)

    await_bytes(k_all.at[pl.ds(WINDOW, length)], in_recv.at[0])

    def turn(tile, carry):
        first = pl.multiple_of(tile * BLOCK, BLOCK)
        k_cols[:, pl.ds(first, BLOCK)] = k_all[pl.ds(first, BLOCK), :].T
        return carry

    lax.fori_loop(0, (length + WINDOW) // BLOCK, turn, 0)

    await_bytes(q_all, in_recv.at[1])

    def weigh(block, carry):
        first = pl.multiple_of(block * BLOCK, BLOCK)
        query = q_all[pl.ds(pl.multiple_of(block * lanes, lanes), lanes), :]
        scores = contract(k_all[pl.ds(first, span), :], query, ((1,), (1,)))
        key_place = lax.broadcasted_iota(jnp.int32, (BLOCK, lanes), 0)
        lane = lax.broadcasted_iota(jnp.int32, (BLOCK, lanes), 1)
        query_place = lane // (CHUNK * per_group) * CHUNK + lane % CHUNK
        tops = []
        for tile in range(tiles):
            part = scores[tile * BLOCK : (tile + 1) * BLOCK, :]
            if tile == 0:
                part = jnp.where(key_place > query_place, part, -BIG)
            if tile == tiles - 1:
                part = jnp.where(key_place <= query_place, part, -BIG)
            weights[block, tile * BLOCK : (tile + 1) * BLOCK, :] = part
            top = jnp.max(part, axis=0, keepdims=True)
            tops.append(jnp.where(tile + block >= tiles - 1, top, -BIG))
        row_max = functools.reduce(jnp.maximum, tops)
        total = jnp.zeros((1, lanes), F32)
        for tile in range(tiles):
            level = jnp.where(tile + block >= tiles - 1, row_max, BIG)
            part = weights[block, tile * BLOCK : (tile + 1) * BLOCK, :]
            part = jnp.exp2((part - level) * exponent_scale)
            weights[block, tile * BLOCK : (tile + 1) * BLOCK, :] = part
            total = total + jnp.sum(part, axis=0, keepdims=True)
        norms[block] = 1.0 / total
        return carry

    lax.fori_loop(0, blocks, weigh, 0)

    await_bytes(v_all.at[pl.ds(WINDOW, length)], in_recv.at[2])
    await_bytes(g_all, in_recv.at[3])

    group_blocks = blocks // side

    def block_of(step):
        row = (my_x + my_y + 1 + step // group_blocks) % side
        return row * group_blocks + (my_y + step) % group_blocks

    def send_query_grads(who):
        source = dq_all.at[pl.ds(who * rows * per_group, rows * per_group)]

        @pl.when(who == me)
        def _():
            pltpu.make_async_copy(source, dq_back.at[me], out_recv.at[0]).start()

        @pl.when(who != me)
        def _():
            pltpu.make_async_remote_copy(
                src_ref=source,
                dst_ref=dq_back.at[me],
                send_sem=out_send.at[0],
                recv_sem=out_recv.at[0],
                device_id=(section, who),
                device_id_type=MESH,
            ).start()

    def release(step):
        turn = step % group_blocks
        place = (my_y + step) % group_blocks
        row = block_of(step) // group_blocks * side

        def done(other):
            return (other + group_blocks - my_y) % group_blocks < turn

        @pl.when((place > 0) & done(place + group_blocks - 1))
        def _():
            send_query_grads(row + place - 1)

        @pl.when((place < side) & done(place + 1))
        def _():
            send_query_grads(row + place)

    def places(step):
        block = block_of(step)
        window = pl.ds(pl.multiple_of(block * BLOCK, BLOCK), span)
        return block, window, pl.ds(pl.multiple_of(block * lanes, lanes), lanes)

    tile_cuts = [slice(tile * BLOCK, (tile + 1) * BLOCK) for tile in range(tiles)]

    def look_ahead(step, products_out):
        block, window, band = places(step)
        products = contract(v_all[window, :], g_all[band, :], ((1,), (1,)))
        row_dot = jnp.zeros((1, lanes), F32)
        for cut in tile_cuts:
            part = products[cut, :]
            products_out[cut, :] = part
            row_dot = row_dot + jnp.sum(
                weights[block, cut, :] * part, axis=0, keepdims=True
            )
            yield row_dot * norms[block]

    def grads(step, after, products_in, products_out, row_dot):
        block, window, band = places(step)
        norm = norms[block]
        ahead_dots = look_ahead(after, products_out)
        for cut in tile_cuts:
            next_dot = next(ahead_dots)
            grad_scores[cut, :] = (
                weights[block, cut, :] * ((products_in[cut, :] - row_dot) * norm)
            ).astype(BF16)
        dk_sum[window, :] += contract(grad_scores[...], q_all[band, :], ((1,), (0,)))
        turned = contract(k_cols[:, window], grad_scores[...], ((1,), (0,)))
        dq_all[band, :] = (turned * query_scale).T.astype(BF16)
        return next_dot

    def two_blocks(pair, row_dot):
        step = 2 * pair
        last = blocks - 1
        row_dot = grads(step, step + 1, grad_probs, next_probs, row_dot)
        row_dot = grads(
            step + 1, jnp.minimum(step + 2, last), next_probs, grad_probs, row_dot
        )

        @pl.when(pair > 0)
        def _():
            release(step - 1)

        release(step)
        return row_dot

    first_dot = list(look_ahead(0, grad_probs))[-1]
    lax.fori_loop(0, blocks // 2, two_blocks, first_dot)
    release(blocks - 1)

    def finish(total, result, scale):
        def one(block, carry):
            here = pl.ds(pl.multiple_of(block * BLOCK, BLOCK), BLOCK)
            there = pl.ds(pl.multiple_of(WINDOW + block * BLOCK, BLOCK), BLOCK)
            result[here, :] = (total[there, :] * scale).astype(BF16)
            return carry

        lax.fori_loop(0, blocks, one, 0)

    def outbound(number, source, target):
        def send(step, carry):
            who = peer(step)
            mine = source.at[pl.ds(who * rows, rows)]

            @pl.when(step == 0)
            def _():
                pltpu.make_async_copy(mine, target.at[me], out_recv.at[number]).start()

            @pl.when(step > 0)
            def _():
                pltpu.make_async_remote_copy(
                    src_ref=mine,
                    dst_ref=target.at[me],
                    send_sem=out_send.at[number],
                    recv_sem=out_recv.at[number],
                    device_id=(section, who),
                    device_id_type=MESH,
                ).start()

            return carry

        lax.fori_loop(0, members, send, 0)

    finish(dk_sum, dk_all, query_scale)
    outbound(2, dk_all, dk_back)

    def value_grads(block, carry):
        first = pl.multiple_of(block * BLOCK, BLOCK)
        band = pl.ds(pl.multiple_of(block * lanes, lanes), lanes)
        dv_sum[pl.ds(first, span), :] += contract(
            (weights[block] * norms[block]).astype(BF16),
            g_all[band, :],
            ((1,), (0,)),
        )
        return carry

    lax.fori_loop(0, blocks, value_grads, 0)
    finish(dv_sum, dv_all, 1.0)
    outbound(1, dv_all, dv_back)

    def others(buffer):
        size = buffer.shape[0] // members
        return buffer.at[pl.ds(0, size * (members - 1))]

    await_bytes(others(k_ready), in_send.at[0])
    await_bytes(others(q_ready), in_send.at[1])
    await_bytes(others(v_ready), in_send.at[2])
    await_bytes(g_ready, in_send.at[3])
    await_bytes(dq_back, out_recv.at[0])
    by_row(dq_back, dq_out)
    await_bytes(dk_back, out_recv.at[2])
    by_row(dk_back, dk_out)
    await_bytes(others(dq_all), out_send.at[0])
    await_bytes(others(dk_all), out_send.at[2])
    await_bytes(dv_back, out_recv.at[1])
    by_row(dv_back, dv_out)
    await_bytes(others(dv_all), out_send.at[1])


def solution(mesh):
    sections, members = mesh.shape["section"], mesh.shape["ctx"]

    def body(queries, key_rows, stored_value_rows, grad_out):
        _, rows, heads, width = queries.shape
        groups = key_rows.shape[2]
        per_group = heads // groups
        length = rows * members
        blocks = length // BLOCK
        span = WINDOW + BLOCK
        lanes = per_group * BLOCK
        outside = pl.BlockSpec(memory_space=pltpu.HBM)
        inside = pl.BlockSpec(memory_space=pltpu.VMEM)
        q_row, kv_row = (rows, heads, width), (rows, groups, width)
        q_sent = (groups, rows * per_group, width)
        kv_sent = (groups, rows, width)
        half = functools.partial(pltpu.VMEM, dtype=BF16)
        full = functools.partial(pltpu.VMEM, dtype=F32)
        dq, dk, dv = pl.pallas_call(
            functools.partial(kernel, sections, members),
            out_shape=tuple(
                jax.ShapeDtypeStruct(shape, BF16) for shape in (q_row, kv_row, kv_row)
            ),
            in_specs=[outside] * 4,
            out_specs=(inside,) * 3,
            scratch_shapes=[
                half((length * per_group, width)),
                half((length + WINDOW, width)),
                half((length + WINDOW, width)),
                half((length * per_group, width)),
                half((width, length + WINDOW)),
                full((blocks, span, lanes)),
                full((blocks, 1, lanes)),
                full((span, lanes)),
                full((span, lanes)),
                half((span, lanes)),
                full((length + WINDOW, width)),
                full((length + WINDOW, width)),
                half((length * per_group, width)),
                half((length, width)),
                half((length, width)),
                half(q_row),
                half(kv_row),
                half(kv_row),
                half(q_row),
                half(q_sent),
                half(kv_sent),
                half(kv_sent),
                half(q_sent),
                half(q_sent),
                half(kv_sent),
                half(kv_sent),
                full((CHUNK * heads, width)),
                pltpu.SemaphoreType.DMA((4,)),
                pltpu.SemaphoreType.DMA((4,)),
                pltpu.SemaphoreType.DMA((4,)),
                pltpu.SemaphoreType.DMA((3,)),
                pltpu.SemaphoreType.DMA((3,)),
            ],
            compiler_params=pltpu.CompilerParams(
                collective_id=0, has_side_effects=True, vmem_limit_bytes=51 << 20
            ),
            name="relay_attention_backward",
        )(
            *(
                pltpu.with_memory_space_constraint(array, pltpu.HBM)
                for array in (
                    queries[0],
                    key_rows[0],
                    stored_value_rows[0],
                    grad_out[0],
                )
            ),
        )
        return dq[None], dk[None], dv[None]

    spec = P("section", "ctx", None, None)
    return jax.shard_map(
        body, mesh=mesh, in_specs=(spec,) * 4, out_specs=(spec,) * 3, check_vma=False
    )
```

```python
import functools
import math

import jax
import jax.numpy as jnp
from jax import lax
from jax.experimental import pallas as pl
from jax.experimental.pallas import tpu as pltpu
from jax.sharding import PartitionSpec as P

MESH = pl.DeviceIdType.MESH
WINDOW = 1024
BLOCK = 128
CHUNK = 32
BIG = 1e30
query_scale = 168.0 ** (-0.5)
exponent_scale = query_scale * math.log2(math.e)

F32 = jnp.float32
BF16 = jnp.bfloat16


def contract(left, right, dims):
    return lax.dot_general(left, right, (dims, ((), ())), preferred_element_type=F32)


def kernel(
    sections,
    members,
    q_hbm,
    k_hbm,
    v_hbm,
    g_hbm,
    dq_out,
    dk_out,
    dv_out,
    q_all,
    k_all,
    v_all,
    g_all,
    k_cols,
    weights,
    norms,
    grad_probs,
    next_probs,
    grad_scores,
    dk_sum,
    dv_sum,
    dq_all,
    dk_all,
    dv_all,
    q_raw,
    k_raw,
    v_raw,
    g_raw,
    q_ready,
    k_ready,
    v_ready,
    g_ready,
    dq_back,
    dk_back,
    dv_back,
    wide,
    load_sem,
    in_send,
    in_recv,
    out_send,
    out_recv,
):
    section = lax.axis_index("section")
    me = lax.axis_index("ctx")
    side = math.isqrt(members)
    my_x, my_y = me // side, me % side
    rows = q_hbm.shape[0]
    length = rows * members
    heads, groups = q_hbm.shape[1], k_hbm.shape[1]
    per_group = heads // groups
    blocks = length // BLOCK
    tiles = WINDOW // BLOCK + 1
    span = WINDOW + BLOCK
    lanes = per_group * BLOCK
    behind = (section + sections - 1) % sections
    ahead = (section + 1) % sections

    def peer(step):
        x = (my_x + step) % side
        y = (my_y + step // side + step) % side
        return x * side + y

    loads = [
        pltpu.make_async_copy(source, raw, load_sem.at[number])
        for number, (source, raw) in enumerate(
            ((k_hbm, k_raw), (q_hbm, q_raw), (v_hbm, v_raw), (g_hbm, g_raw))
        )
    ]
    for load in loads:
        load.start()

    barrier = pltpu.get_barrier_semaphore()

    def greet(step, carry):
        pl.semaphore_signal(
            barrier, inc=1, device_id=(ahead, peer(step)), device_id_type=MESH
        )

        @pl.when(step > 0)
        def _():
            pl.semaphore_signal(
                barrier, inc=1, device_id=(section, peer(step)), device_id_type=MESH
            )

        return carry

    lax.fori_loop(0, members, greet, 0)

    def by_group(raw, ready):
        count = raw.shape[1]
        each = count // groups
        flat = raw.reshape(rows * count, raw.shape[2])

        def one(chunk, carry):
            here = pl.ds(pl.multiple_of(chunk * CHUNK * count, CHUNK), CHUNK * count)
            wide[0 : CHUNK * count, :] = flat[here, :].astype(F32)
            for head in range(count):
                first = (chunk * each + head % each) * CHUNK
                ready[head // each, pl.ds(pl.multiple_of(first, CHUNK), CHUNK), :] = (
                    wide[pl.ds(head, CHUNK, stride=count), :].astype(BF16)
                )
            return carry

        lax.fori_loop(0, rows // CHUNK, one, 0)

    def by_row(back, out):
        count = out.shape[1]
        each = count // groups
        flat = out.reshape(rows * count, out.shape[2])

        def one(chunk, carry):
            for head in range(count):
                first = (chunk * each + head % each) * CHUNK
                wide[pl.ds(head, CHUNK, stride=count), :] = back[
                    head // each, pl.ds(pl.multiple_of(first, CHUNK), CHUNK), :
                ].astype(F32)
            here = pl.ds(pl.multiple_of(chunk * CHUNK * count, CHUNK), CHUNK * count)
            flat[here, :] = wide[0 : CHUNK * count, :].astype(BF16)
            return carry

        lax.fori_loop(0, rows // CHUNK, one, 0)

    loads[0].wait()
    by_group(k_raw, k_ready)
    pl.semaphore_wait(barrier, 2 * members - 1)

    def inbound(number, ready, buffer, pad, target_section, parts):
        size = ready.shape[1]
        piece = size // parts

        def send(turn, carry):
            step = turn % members
            first = turn // members * piece
            who = peer(step)
            mine = ready.at[who, pl.ds(first, piece)]
            there = buffer.at[pl.ds(pad + me * size + first, piece)]
            near = (step == 0) & (target_section == section)

            @pl.when(near)
            def _():
                pltpu.make_async_copy(mine, there, in_recv.at[number]).start()

            @pl.when(jnp.logical_not(near))
            def _():
                pltpu.make_async_remote_copy(
                    src_ref=mine,
                    dst_ref=there,
                    send_sem=in_send.at[number],
                    recv_sem=in_recv.at[number],
                    device_id=(target_section, who),
                    device_id_type=MESH,
                ).start()

            return carry

        lax.fori_loop(0, members * parts, send, 0)

    inbound(0, k_ready, k_all, WINDOW, section, 2)
    loads[1].wait()
    by_group(q_raw, q_ready)
    inbound(1, q_ready, q_all, 0, section, 4)
    loads[2].wait()
    by_group(v_raw, v_ready)
    inbound(2, v_ready, v_all, WINDOW, section, 2)
    loads[3].wait()
    by_group(g_raw, g_ready)
    inbound(3, g_ready, g_all, 0, behind, 4)

    def await_bytes(view, semaphore):
        pltpu.make_async_copy(view, view, semaphore).wait()

    k_all[0:WINDOW, :] = jnp.zeros((WINDOW, k_all.shape[1]), BF16)
    v_all[0:WINDOW, :] = jnp.zeros((WINDOW, v_all.shape[1]), BF16)
    dk_sum[...] = jnp.zeros(dk_sum.shape, F32)
    dv_sum[...] = jnp.zeros(dv_sum.shape, F32)

    early = tiles // 2 + 1
    for block in range(early):
        weights[block, 0 : (tiles - early) * BLOCK, :] = jnp.zeros(
            ((tiles - early) * BLOCK, lanes), F32
        )

    await_bytes(k_all.at[pl.ds(WINDOW, length)], in_recv.at[0])

    def turn(tile, carry):
        first = pl.multiple_of(tile * BLOCK, BLOCK)
        k_cols[:, pl.ds(first, BLOCK)] = k_all[pl.ds(first, BLOCK), :].T
        return carry

    lax.fori_loop(0, (length + WINDOW) // BLOCK, turn, 0)

    await_bytes(q_all, in_recv.at[1])

    def weigh(first_tile, block, carry):
        first = pl.multiple_of(block * BLOCK, BLOCK)
        query = q_all[pl.ds(pl.multiple_of(block * lanes, lanes), lanes), :]
        start = first_tile * BLOCK
        scores = contract(
            k_all[pl.ds(first + start, span - start), :], query, ((1,), (1,))
        )
        key_place = lax.broadcasted_iota(jnp.int32, (BLOCK, lanes), 0)
        lane = lax.broadcasted_iota(jnp.int32, (BLOCK, lanes), 1)
        query_place = lane // (CHUNK * per_group) * CHUNK + lane % CHUNK
        tops = []
        for tile in range(first_tile, tiles):
            part = scores[tile * BLOCK - start : (tile + 1) * BLOCK - start, :]
            if tile == 0:
                part = jnp.where(key_place > query_place, part, -BIG)
            if tile == tiles - 1:
                part = jnp.where(key_place <= query_place, part, -BIG)
            weights[block, tile * BLOCK : (tile + 1) * BLOCK, :] = part
            top = jnp.max(part, axis=0, keepdims=True)
            tops.append(jnp.where(tile + block >= tiles - 1, top, -BIG))
        row_max = functools.reduce(jnp.maximum, tops)
        total = jnp.zeros((1, lanes), F32)
        for tile in range(first_tile, tiles):
            level = jnp.where(tile + block >= tiles - 1, row_max, BIG)
            part = weights[block, tile * BLOCK : (tile + 1) * BLOCK, :]
            part = jnp.exp2((part - level) * exponent_scale)
            weights[block, tile * BLOCK : (tile + 1) * BLOCK, :] = part
            total = total + jnp.sum(part, axis=0, keepdims=True)
        norms[block] = 1.0 / total
        return carry

    lax.fori_loop(0, early, functools.partial(weigh, tiles - early), 0)
    lax.fori_loop(early, blocks, functools.partial(weigh, 0), 0)

    await_bytes(v_all.at[pl.ds(WINDOW, length)], in_recv.at[2])
    await_bytes(g_all, in_recv.at[3])

    group_blocks = blocks // side

    def block_of(step):
        row = (my_x + my_y + 1 + step // group_blocks) % side
        return row * group_blocks + (my_y + step) % group_blocks

    def send_query_grads(who):
        source = dq_all.at[pl.ds(who * rows * per_group, rows * per_group)]

        @pl.when(who == me)
        def _():
            pltpu.make_async_copy(source, dq_back.at[me], out_recv.at[0]).start()

        @pl.when(who != me)
        def _():
            pltpu.make_async_remote_copy(
                src_ref=source,
                dst_ref=dq_back.at[me],
                send_sem=out_send.at[0],
                recv_sem=out_recv.at[0],
                device_id=(section, who),
                device_id_type=MESH,
            ).start()

    def release(step):
        turn = step % group_blocks
        place = (my_y + step) % group_blocks
        row = block_of(step) // group_blocks * side

        def done(other):
            return (other + group_blocks - my_y) % group_blocks < turn

        @pl.when((place > 0) & done(place + group_blocks - 1))
        def _():
            send_query_grads(row + place - 1)

        @pl.when((place < side) & done(place + 1))
        def _():
            send_query_grads(row + place)

    def places(step):
        block = block_of(step)
        window = pl.ds(pl.multiple_of(block * BLOCK, BLOCK), span)
        return block, window, pl.ds(pl.multiple_of(block * lanes, lanes), lanes)

    tile_cuts = [slice(tile * BLOCK, (tile + 1) * BLOCK) for tile in range(tiles)]

    def look_ahead(step, products_out):
        block, window, band = places(step)
        products = contract(v_all[window, :], g_all[band, :], ((1,), (1,)))
        row_dot = jnp.zeros((1, lanes), F32)
        for cut in tile_cuts:
            part = products[cut, :]
            products_out[cut, :] = part
            row_dot = row_dot + jnp.sum(
                weights[block, cut, :] * part, axis=0, keepdims=True
            )
            yield row_dot * norms[block]

    def grads(step, after, products_in, products_out, row_dot):
        block, window, band = places(step)
        norm = norms[block]
        ahead_dots = look_ahead(after, products_out)
        for cut in tile_cuts:
            next_dot = next(ahead_dots)
            grad_scores[cut, :] = (
                weights[block, cut, :] * ((products_in[cut, :] - row_dot) * norm)
            ).astype(BF16)
        dk_sum[window, :] += contract(grad_scores[...], q_all[band, :], ((1,), (0,)))
        turned = contract(k_cols[:, window], grad_scores[...], ((1,), (0,)))
        dq_all[band, :] = (turned * query_scale).T.astype(BF16)
        return next_dot

    def two_blocks(pair, row_dot):
        step = 2 * pair
        last = blocks - 1
        row_dot = grads(step, step + 1, grad_probs, next_probs, row_dot)
        row_dot = grads(
            step + 1, jnp.minimum(step + 2, last), next_probs, grad_probs, row_dot
        )

        @pl.when(pair > 0)
        def _():
            release(step - 1)

        release(step)
        return row_dot

    first_dot = list(look_ahead(0, grad_probs))[-1]
    lax.fori_loop(0, blocks // 2, two_blocks, first_dot)
    release(blocks - 1)

    def finish(total, result, scale):
        def one(block, carry):
            here = pl.ds(pl.multiple_of(block * BLOCK, BLOCK), BLOCK)
            there = pl.ds(pl.multiple_of(WINDOW + block * BLOCK, BLOCK), BLOCK)
            result[here, :] = (total[there, :] * scale).astype(BF16)
            return carry

        lax.fori_loop(0, blocks, one, 0)

    def outbound(number, source, target):
        def send(step, carry):
            who = peer(step)
            mine = source.at[pl.ds(who * rows, rows)]

            @pl.when(step == 0)
            def _():
                pltpu.make_async_copy(mine, target.at[me], out_recv.at[number]).start()

            @pl.when(step > 0)
            def _():
                pltpu.make_async_remote_copy(
                    src_ref=mine,
                    dst_ref=target.at[me],
                    send_sem=out_send.at[number],
                    recv_sem=out_recv.at[number],
                    device_id=(section, who),
                    device_id_type=MESH,
                ).start()

            return carry

        lax.fori_loop(0, members, send, 0)

    finish(dk_sum, dk_all, query_scale)
    outbound(2, dk_all, dk_back)

    def value_grads(block, carry):
        first = pl.multiple_of(block * BLOCK, BLOCK)
        band = pl.ds(pl.multiple_of(block * lanes, lanes), lanes)
        dv_sum[pl.ds(first, span), :] += contract(
            (weights[block] * norms[block]).astype(BF16),
            g_all[band, :],
            ((1,), (0,)),
        )
        return carry

    lax.fori_loop(0, blocks, value_grads, 0)
    finish(dv_sum, dv_all, 1.0)
    outbound(1, dv_all, dv_back)

    def others(buffer):
        size = buffer.shape[0] // members
        return buffer.at[pl.ds(0, size * (members - 1))]

    await_bytes(others(k_ready), in_send.at[0])
    await_bytes(others(q_ready), in_send.at[1])
    await_bytes(others(v_ready), in_send.at[2])
    await_bytes(g_ready, in_send.at[3])
    await_bytes(dq_back, out_recv.at[0])
    by_row(dq_back, dq_out)
    await_bytes(dk_back, out_recv.at[2])
    by_row(dk_back, dk_out)
    await_bytes(others(dq_all), out_send.at[0])
    await_bytes(others(dk_all), out_send.at[2])
    await_bytes(dv_back, out_recv.at[1])
    by_row(dv_back, dv_out)
    await_bytes(others(dv_all), out_send.at[1])


def settle(*refs):
    sources, targets, semaphores = refs[:3], refs[3:6], refs[6]
    copies = [
        pltpu.make_async_copy(source, target, semaphores.at[number])
        for number, (source, target) in enumerate(zip(sources, targets))
    ]
    for copy in copies:
        copy.start()
    for copy in copies:
        copy.wait()


def solution(mesh):
    sections, members = mesh.shape["section"], mesh.shape["ctx"]

    def body(queries, key_rows, stored_value_rows, grad_out):
        _, rows, heads, width = queries.shape
        groups = key_rows.shape[2]
        per_group = heads // groups
        length = rows * members
        blocks = length // BLOCK
        span = WINDOW + BLOCK
        lanes = per_group * BLOCK
        outside = pl.BlockSpec(memory_space=pltpu.HBM)
        inside = pl.BlockSpec(memory_space=pltpu.VMEM)
        q_row, kv_row = (rows, heads, width), (rows, groups, width)
        q_sent = (groups, rows * per_group, width)
        kv_sent = (groups, rows, width)
        results = tuple(
            jax.ShapeDtypeStruct(shape, BF16) for shape in (q_row, kv_row, kv_row)
        )
        half = functools.partial(pltpu.VMEM, dtype=BF16)
        full = functools.partial(pltpu.VMEM, dtype=F32)
        dq, dk, dv = pl.pallas_call(
            functools.partial(kernel, sections, members),
            out_shape=results,
            in_specs=[outside] * 4,
            out_specs=(inside,) * 3,
            scratch_shapes=[
                half((length * per_group, width)),
                half((length + WINDOW, width)),
                half((length + WINDOW, width)),
                half((length * per_group, width)),
                half((width, length + WINDOW)),
                full((blocks, span, lanes)),
                full((blocks, 1, lanes)),
                full((span, lanes)),
                full((span, lanes)),
                half((span, lanes)),
                full((length + WINDOW, width)),
                full((length + WINDOW, width)),
                half((length * per_group, width)),
                half((length, width)),
                half((length, width)),
                half(q_row),
                half(kv_row),
                half(kv_row),
                half(q_row),
                half(q_sent),
                half(kv_sent),
                half(kv_sent),
                half(q_sent),
                half(q_sent),
                half(kv_sent),
                half(kv_sent),
                full((CHUNK * heads, width)),
                pltpu.SemaphoreType.DMA((4,)),
                pltpu.SemaphoreType.DMA((4,)),
                pltpu.SemaphoreType.DMA((4,)),
                pltpu.SemaphoreType.DMA((3,)),
                pltpu.SemaphoreType.DMA((3,)),
            ],
            compiler_params=pltpu.CompilerParams(
                collective_id=0, has_side_effects=True, vmem_limit_bytes=51 << 20
            ),
            name="relay_attention_backward",
        )(
            *(
                pltpu.with_memory_space_constraint(array, pltpu.HBM)
                for array in (
                    queries[0],
                    key_rows[0],
                    stored_value_rows[0],
                    grad_out[0],
                )
            ),
        )
        dq, dk, dv = pl.pallas_call(
            settle,
            out_shape=results,
            in_specs=[inside] * 3,
            out_specs=(outside,) * 3,
            scratch_shapes=[pltpu.SemaphoreType.DMA((3,))],
            compiler_params=pltpu.CompilerParams(vmem_limit_bytes=1 << 20),
            name="settle",
        )(dq, dk, dv)
        return dq[None], dk[None], dv[None]

    spec = P("section", "ctx", None, None)
    return jax.shard_map(
        body, mesh=mesh, in_specs=(spec,) * 4, out_specs=(spec,) * 3, check_vma=False
    )
```

```python
import functools
import math

import jax
import jax.numpy as jnp
from jax import lax
from jax.experimental import pallas as pl
from jax.experimental.pallas import tpu as pltpu
from jax.sharding import PartitionSpec as P

MESH = pl.DeviceIdType.MESH
WINDOW = 1024
BLOCK = 128
CHUNK = 32
BIG = 1e30
query_scale = 168.0 ** (-0.5)
exponent_scale = query_scale * math.log2(math.e)

F32 = jnp.float32
BF16 = jnp.bfloat16


def contract(left, right, dims):
    return lax.dot_general(left, right, (dims, ((), ())), preferred_element_type=F32)


def kernel(
    sections,
    members,
    q_hbm,
    k_hbm,
    v_hbm,
    g_hbm,
    dq_out,
    dk_out,
    dv_out,
    q_all,
    k_all,
    v_all,
    g_all,
    k_cols,
    weights,
    norms,
    grad_probs,
    next_probs,
    grad_scores,
    dk_sum,
    dv_sum,
    dq_all,
    dk_all,
    dv_all,
    q_raw,
    k_raw,
    v_raw,
    g_raw,
    q_ready,
    k_ready,
    v_ready,
    g_ready,
    dq_back,
    dk_back,
    dv_back,
    wide,
    load_sem,
    in_send,
    in_recv,
    out_send,
    out_recv,
):
    section = lax.axis_index("section")
    me = lax.axis_index("ctx")
    side = math.isqrt(members)
    my_x, my_y = me // side, me % side
    rows = q_hbm.shape[0]
    length = rows * members
    heads, groups = q_hbm.shape[1], k_hbm.shape[1]
    per_group = heads // groups
    blocks = length // BLOCK
    tiles = WINDOW // BLOCK + 1
    span = WINDOW + BLOCK
    lanes = per_group * BLOCK
    behind = (section + sections - 1) % sections
    ahead = (section + 1) % sections

    def peer(step):
        x = (my_x + step // side + step) % side
        y = (my_y + step) % side
        return x * side + y

    loads = [
        pltpu.make_async_copy(source, raw, load_sem.at[number])
        for number, (source, raw) in enumerate(
            ((k_hbm, k_raw), (q_hbm, q_raw), (v_hbm, v_raw), (g_hbm, g_raw))
        )
    ]
    for load in loads:
        load.start()

    barrier = pltpu.get_barrier_semaphore()

    def greet(step, carry):
        pl.semaphore_signal(
            barrier, inc=1, device_id=(ahead, peer(step)), device_id_type=MESH
        )

        @pl.when(step > 0)
        def _():
            pl.semaphore_signal(
                barrier, inc=1, device_id=(section, peer(step)), device_id_type=MESH
            )

        return carry

    lax.fori_loop(0, members, greet, 0)

    def by_group(raw, ready):
        count = raw.shape[1]
        each = count // groups
        flat = raw.reshape(rows * count, raw.shape[2])

        def one(chunk, carry):
            here = pl.ds(pl.multiple_of(chunk * CHUNK * count, CHUNK), CHUNK * count)
            wide[0 : CHUNK * count, :] = flat[here, :].astype(F32)
            for head in range(count):
                first = (chunk * each + head % each) * CHUNK
                ready[head // each, pl.ds(pl.multiple_of(first, CHUNK), CHUNK), :] = (
                    wide[pl.ds(head, CHUNK, stride=count), :].astype(BF16)
                )
            return carry

        lax.fori_loop(0, rows // CHUNK, one, 0)

    def by_row(back, out):
        count = out.shape[1]
        each = count // groups
        flat = out.reshape(rows * count, out.shape[2])

        def one(chunk, carry):
            for head in range(count):
                first = (chunk * each + head % each) * CHUNK
                wide[pl.ds(head, CHUNK, stride=count), :] = back[
                    head // each, pl.ds(pl.multiple_of(first, CHUNK), CHUNK), :
                ].astype(F32)
            here = pl.ds(pl.multiple_of(chunk * CHUNK * count, CHUNK), CHUNK * count)
            flat[here, :] = wide[0 : CHUNK * count, :].astype(BF16)
            return carry

        lax.fori_loop(0, rows // CHUNK, one, 0)

    loads[0].wait()
    by_group(k_raw, k_ready)
    pl.semaphore_wait(barrier, 2 * members - 1)

    def inbound(number, ready, buffer, pad, target_section, parts):
        size = ready.shape[1]
        piece = size // parts

        def send(turn, carry):
            step = turn % members
            first = turn // members * piece
            who = peer(step)
            mine = ready.at[who, pl.ds(first, piece)]
            there = buffer.at[pl.ds(pad + me * size + first, piece)]
            near = (step == 0) & (target_section == section)

            @pl.when(near)
            def _():
                pltpu.make_async_copy(mine, there, in_recv.at[number]).start()

            @pl.when(jnp.logical_not(near))
            def _():
                pltpu.make_async_remote_copy(
                    src_ref=mine,
                    dst_ref=there,
                    send_sem=in_send.at[number],
                    recv_sem=in_recv.at[number],
                    device_id=(target_section, who),
                    device_id_type=MESH,
                ).start()

            return carry

        lax.fori_loop(0, members * parts, send, 0)

    inbound(0, k_ready, k_all, WINDOW, section, 2)
    loads[1].wait()
    by_group(q_raw, q_ready)
    inbound(1, q_ready, q_all, 0, section, 4)
    loads[2].wait()
    by_group(v_raw, v_ready)
    inbound(2, v_ready, v_all, WINDOW, section, 2)
    loads[3].wait()
    by_group(g_raw, g_ready)
    inbound(3, g_ready, g_all, 0, behind, 4)

    def await_bytes(view, semaphore):
        pltpu.make_async_copy(view, view, semaphore).wait()

    k_all[0:WINDOW, :] = jnp.zeros((WINDOW, k_all.shape[1]), BF16)
    v_all[0:WINDOW, :] = jnp.zeros((WINDOW, v_all.shape[1]), BF16)
    dk_sum[...] = jnp.zeros(dk_sum.shape, F32)
    dv_sum[...] = jnp.zeros(dv_sum.shape, F32)

    early = tiles // 2 + 1
    for block in range(early):
        weights[block, 0 : (tiles - early) * BLOCK, :] = jnp.zeros(
            ((tiles - early) * BLOCK, lanes), F32
        )

    await_bytes(k_all.at[pl.ds(WINDOW, length)], in_recv.at[0])

    def turn(tile, carry):
        first = pl.multiple_of(tile * BLOCK, BLOCK)
        k_cols[:, pl.ds(first, BLOCK)] = k_all[pl.ds(first, BLOCK), :].T
        return carry

    lax.fori_loop(0, (length + WINDOW) // BLOCK, turn, 0)

    await_bytes(q_all, in_recv.at[1])

    def weigh(first_tile, block, carry):
        first = pl.multiple_of(block * BLOCK, BLOCK)
        query = q_all[pl.ds(pl.multiple_of(block * lanes, lanes), lanes), :]
        start = first_tile * BLOCK
        scores = contract(
            k_all[pl.ds(first + start, span - start), :], query, ((1,), (1,))
        )
        key_place = lax.broadcasted_iota(jnp.int32, (BLOCK, lanes), 0)
        lane = lax.broadcasted_iota(jnp.int32, (BLOCK, lanes), 1)
        query_place = lane // (CHUNK * per_group) * CHUNK + lane % CHUNK
        tops = []
        for tile in range(first_tile, tiles):
            part = scores[tile * BLOCK - start : (tile + 1) * BLOCK - start, :]
            if tile == 0:
                part = jnp.where(key_place > query_place, part, -BIG)
            if tile == tiles - 1:
                part = jnp.where(key_place <= query_place, part, -BIG)
            weights[block, tile * BLOCK : (tile + 1) * BLOCK, :] = part
            top = jnp.max(part, axis=0, keepdims=True)
            tops.append(jnp.where(tile + block >= tiles - 1, top, -BIG))
        row_max = functools.reduce(jnp.maximum, tops)
        total = jnp.zeros((1, lanes), F32)
        for tile in range(first_tile, tiles):
            level = jnp.where(tile + block >= tiles - 1, row_max, BIG)
            part = weights[block, tile * BLOCK : (tile + 1) * BLOCK, :]
            part = jnp.exp2((part - level) * exponent_scale)
            weights[block, tile * BLOCK : (tile + 1) * BLOCK, :] = part
            total = total + jnp.sum(part, axis=0, keepdims=True)
        norms[block] = 1.0 / total
        return carry

    lax.fori_loop(0, early, functools.partial(weigh, tiles - early), 0, unroll=True)
    lax.fori_loop(early, blocks, functools.partial(weigh, 0), 0, unroll=3)

    await_bytes(v_all.at[pl.ds(WINDOW, length)], in_recv.at[2])
    await_bytes(g_all, in_recv.at[3])

    group_blocks = blocks // side

    def block_of(step):
        row = (my_x + my_y + 1 + step // group_blocks) % side
        return row * group_blocks + (my_y + step) % group_blocks

    def send_query_grads(who):
        source = dq_all.at[pl.ds(who * rows * per_group, rows * per_group)]

        @pl.when(who == me)
        def _():
            pltpu.make_async_copy(source, dq_back.at[me], out_recv.at[0]).start()

        @pl.when(who != me)
        def _():
            pltpu.make_async_remote_copy(
                src_ref=source,
                dst_ref=dq_back.at[me],
                send_sem=out_send.at[0],
                recv_sem=out_recv.at[0],
                device_id=(section, who),
                device_id_type=MESH,
            ).start()

    def release(step):
        turn = step % group_blocks
        place = (my_y + step) % group_blocks
        row = block_of(step) // group_blocks * side

        def done(other):
            return (other + group_blocks - my_y) % group_blocks < turn

        @pl.when((place > 0) & done(place + group_blocks - 1))
        def _():
            send_query_grads(row + place - 1)

        @pl.when((place < side) & done(place + 1))
        def _():
            send_query_grads(row + place)

    def places(step):
        block = block_of(step)
        window = pl.ds(pl.multiple_of(block * BLOCK, BLOCK), span)
        return block, window, pl.ds(pl.multiple_of(block * lanes, lanes), lanes)

    tile_cuts = [slice(tile * BLOCK, (tile + 1) * BLOCK) for tile in range(tiles)]

    def look_ahead(step, products_out):
        block, window, band = places(step)
        products = contract(v_all[window, :], g_all[band, :], ((1,), (1,)))
        row_dot = jnp.zeros((1, lanes), F32)
        for cut in tile_cuts:
            part = products[cut, :]
            products_out[cut, :] = part
            row_dot = row_dot + jnp.sum(
                weights[block, cut, :] * part, axis=0, keepdims=True
            )
            yield row_dot * norms[block]

    def grads(step, after, products_in, products_out, row_dot):
        block, window, band = places(step)
        norm = norms[block]
        ahead_dots = look_ahead(after, products_out)
        for cut in tile_cuts:
            next_dot = next(ahead_dots)
            grad_scores[cut, :] = (
                weights[block, cut, :] * ((products_in[cut, :] - row_dot) * norm)
            ).astype(BF16)
        dk_sum[window, :] += contract(grad_scores[...], q_all[band, :], ((1,), (0,)))
        turned = contract(k_cols[:, window], grad_scores[...], ((1,), (0,)))
        dq_all[band, :] = (turned * query_scale).T.astype(BF16)
        return next_dot

    def four_blocks(turn, row_dot):
        step = 4 * turn
        last = blocks - 1
        probs = (grad_probs, next_probs)
        for offset in range(4):
            row_dot = grads(
                step + offset,
                jnp.minimum(step + offset + 1, last),
                probs[offset % 2],
                probs[1 - offset % 2],
                row_dot,
            )

        @pl.when(turn > 0)
        def _():
            release(step - 1)

        for offset in range(3):
            release(step + offset)
        return row_dot

    first_dot = list(look_ahead(0, grad_probs))[-1]
    lax.fori_loop(0, blocks // 4, four_blocks, first_dot)
    release(blocks - 1)

    def finish(total, result, scale):
        def one(block, carry):
            here = pl.ds(pl.multiple_of(block * BLOCK, BLOCK), BLOCK)
            there = pl.ds(pl.multiple_of(WINDOW + block * BLOCK, BLOCK), BLOCK)
            result[here, :] = (total[there, :] * scale).astype(BF16)
            return carry

        lax.fori_loop(0, blocks, one, 0)

    def outbound(number, source, target):
        def send(step, carry):
            who = peer(step)
            mine = source.at[pl.ds(who * rows, rows)]

            @pl.when(step == 0)
            def _():
                pltpu.make_async_copy(mine, target.at[me], out_recv.at[number]).start()

            @pl.when(step > 0)
            def _():
                pltpu.make_async_remote_copy(
                    src_ref=mine,
                    dst_ref=target.at[me],
                    send_sem=out_send.at[number],
                    recv_sem=out_recv.at[number],
                    device_id=(section, who),
                    device_id_type=MESH,
                ).start()

            return carry

        lax.fori_loop(0, members, send, 0)

    finish(dk_sum, dk_all, query_scale)
    outbound(2, dk_all, dk_back)

    def value_grads(block, carry):
        first = pl.multiple_of(block * BLOCK, BLOCK)
        band = pl.ds(pl.multiple_of(block * lanes, lanes), lanes)
        dv_sum[pl.ds(first, span), :] += contract(
            (weights[block] * norms[block]).astype(BF16),
            g_all[band, :],
            ((1,), (0,)),
        )
        return carry

    lax.fori_loop(0, blocks, value_grads, 0, unroll=2)
    finish(dv_sum, dv_all, 1.0)
    outbound(1, dv_all, dv_back)

    def others(buffer):
        size = buffer.shape[0] // members
        return buffer.at[pl.ds(0, size * (members - 1))]

    await_bytes(others(k_ready), in_send.at[0])
    await_bytes(others(q_ready), in_send.at[1])
    await_bytes(others(v_ready), in_send.at[2])
    await_bytes(g_ready, in_send.at[3])
    await_bytes(dq_back, out_recv.at[0])
    by_row(dq_back, dq_out)
    await_bytes(dk_back, out_recv.at[2])
    by_row(dk_back, dk_out)
    await_bytes(others(dq_all), out_send.at[0])
    await_bytes(others(dk_all), out_send.at[2])
    await_bytes(dv_back, out_recv.at[1])
    by_row(dv_back, dv_out)
    await_bytes(others(dv_all), out_send.at[1])


def settle(*refs):
    sources, targets, semaphores = refs[:3], refs[3:6], refs[6]
    copies = [
        pltpu.make_async_copy(source, target, semaphores.at[number])
        for number, (source, target) in enumerate(zip(sources, targets))
    ]
    for copy in copies:
        copy.start()
    for copy in copies:
        copy.wait()


def solution(mesh):
    sections, members = mesh.shape["section"], mesh.shape["ctx"]

    def body(queries, key_rows, stored_value_rows, grad_out):
        _, rows, heads, width = queries.shape
        groups = key_rows.shape[2]
        per_group = heads // groups
        length = rows * members
        blocks = length // BLOCK
        span = WINDOW + BLOCK
        lanes = per_group * BLOCK
        outside = pl.BlockSpec(memory_space=pltpu.HBM)
        inside = pl.BlockSpec(memory_space=pltpu.VMEM)
        q_row, kv_row = (rows, heads, width), (rows, groups, width)
        q_sent = (groups, rows * per_group, width)
        kv_sent = (groups, rows, width)
        results = tuple(
            jax.ShapeDtypeStruct(shape, BF16) for shape in (q_row, kv_row, kv_row)
        )
        half = functools.partial(pltpu.VMEM, dtype=BF16)
        full = functools.partial(pltpu.VMEM, dtype=F32)
        dq, dk, dv = pl.pallas_call(
            functools.partial(kernel, sections, members),
            out_shape=results,
            in_specs=[outside] * 4,
            out_specs=(inside,) * 3,
            scratch_shapes=[
                half((length * per_group, width)),
                half((length + WINDOW, width)),
                half((length + WINDOW, width)),
                half((length * per_group, width)),
                half((width, length + WINDOW)),
                full((blocks, span, lanes)),
                full((blocks, 1, lanes)),
                full((span, lanes)),
                full((span, lanes)),
                half((span, lanes)),
                full((length + WINDOW, width)),
                full((length + WINDOW, width)),
                half((length * per_group, width)),
                half((length, width)),
                half((length, width)),
                half(q_row),
                half(kv_row),
                half(kv_row),
                half(q_row),
                half(q_sent),
                half(kv_sent),
                half(kv_sent),
                half(q_sent),
                half(q_sent),
                half(kv_sent),
                half(kv_sent),
                full((CHUNK * heads, width)),
                pltpu.SemaphoreType.DMA((4,)),
                pltpu.SemaphoreType.DMA((4,)),
                pltpu.SemaphoreType.DMA((4,)),
                pltpu.SemaphoreType.DMA((3,)),
                pltpu.SemaphoreType.DMA((3,)),
            ],
            compiler_params=pltpu.CompilerParams(
                collective_id=0, has_side_effects=True, vmem_limit_bytes=51 << 20
            ),
            name="relay_attention_backward",
        )(
            *(
                pltpu.with_memory_space_constraint(array, pltpu.HBM)
                for array in (
                    queries[0],
                    key_rows[0],
                    stored_value_rows[0],
                    grad_out[0],
                )
            ),
        )
        dq, dk, dv = pl.pallas_call(
            settle,
            out_shape=results,
            in_specs=[inside] * 3,
            out_specs=(outside,) * 3,
            scratch_shapes=[pltpu.SemaphoreType.DMA((3,))],
            compiler_params=pltpu.CompilerParams(vmem_limit_bytes=1 << 20),
            name="settle",
        )(dq, dk, dv)
        return dq[None], dk[None], dv[None]

    spec = P("section", "ctx", None, None)
    return jax.shard_map(
        body, mesh=mesh, in_specs=(spec,) * 4, out_specs=(spec,) * 3, check_vma=False
    )
```
